32 devices in a mesh: shard: 2 (over y), tensor: 4 (over x, core), section: 4 (over z).
Axes of the slice: x: 2, y: 2, z: 4, core: 2. Of those that a mesh axis runs over, the one named last changes fastest.
Arguments:
- grad_parts: float32 [2, 4, 4, 1152, 1024], P('shard', 'tensor', 'section'), may hold values from -1 to 1
- master: float32 [1152, 16, 1024], P(('tensor', 'section'), 'shard'), may hold values from -0.1875 to 0.1875
- owner_map: int32 [4, 4], replicated, may hold values from 0 to 1, as said below
- left_factor: float32 [16, 1152, 1152], P('shard', ('tensor', 'section')), may hold values from -1.2 to 11.2, as said below
- right_factor: float32 [16, 1024, 1024], P('shard', ('tensor', 'section')), may hold values from -1.2 to 11.2, as said below
- left_basis: float32 [16, 1152, 1152], P('shard', ('tensor', 'section')), may hold values from -0.1875 to 0.1875
- right_basis: float32 [16, 1024, 1024], P('shard', None, ('tensor', 'section')), may hold values from -0.1875 to 0.1875
- moment_one: float32 [16, 1152, 1024], P('shard', ('tensor', 'section')), may hold values from -3 to 3
- moment_two: float32 [16, 1152, 1024], P('shard', ('tensor', 'section')), may hold values from 0.01 to 0.5
Outputs:
- new_master: float32 [1152, 16, 1024], P(('tensor', 'section'), 'shard')
- update_dir: float32 [1152, 16, 1024], P(('tensor', 'section'), 'shard')
- new_left: float32 [16, 1152, 1152], P('shard', ('tensor', 'section'))
- new_right: float32 [16, 1024, 1024], P('shard', ('tensor', 'section'))
- new_moment_one: float32 [16, 1152, 1024], P('shard', ('tensor', 'section'))
- new_moment_two: float32 [16, 1152, 1024], P('shard', ('tensor', 'section'))
The draws below stay inside these ranges and needn't reach their ends.
Inputs may be any that keep to these rules, and one draw needn't show every extreme that they name: `owner_map`: each shard index owns exactly 8 matrices. `left_factor`: symmetric in its last two dimensions. `right_factor`: symmetric in its last two dimensions.
All inputs are finite; a program needn't handle non-finite values.
Results may differ from the reference program's by a relative error of at most 0.0003.
Values sent between devices are 32-bit elements; how exact they have to be, the bound alone decides.
A program may use at most 448 MiB of HBM per device.

```python
import math
import jax
import jax.numpy as jnp
from jax import lax

D = 1024
BLOCK = 1152
BLOCKS = 4
LAYERS = 4
MATS = 16
OWN = 8
N_SHARD = 2


def symmetric_draw(key, number, extent):
    key_one, key_two = jax.random.split(key)
    noise_draw = jax.random.truncated_normal(key_one, -4.0, 4.0, (number, extent, extent), jnp.float32)
    symmetric = 0.5 * (noise_draw + jnp.swapaxes(noise_draw, 1, 2))
    diagonal = jnp.exp(jax.random.uniform(key_two, (number, 1, extent), jnp.float32, 0.0, 2.3))
    identity = (jnp.arange(extent)[:, None] == jnp.arange(extent)[None, :]).astype(jnp.float32)
    return 0.3 * symmetric + diagonal * identity


def draw_left_factor(key, part):
    return symmetric_draw(jax.random.fold_in(key, 11), MATS, BLOCK)


def draw_right_factor(key, part):
    return symmetric_draw(jax.random.fold_in(key, 23), MATS, D)


def draw_owner_map(key, part):
    shuffled = jax.random.permutation(jax.random.fold_in(key, 37), MATS).astype(jnp.int32)
    return (shuffled // OWN).astype(jnp.int32).reshape(BLOCKS, LAYERS)


def spiked(drawn, key, source, target, parts, factor):
    def block_of(axis_at):
        return (jnp.arange(drawn.shape[axis_at]) // (drawn.shape[axis_at] // parts)).reshape((-1,) + (1,) * (drawn.ndim - 1 - axis_at))

    one_side = jax.random.permutation(key, parts)[block_of(target)]
    far = (block_of(target) + parts // 2) % parts
    return jnp.where((block_of(source) == one_side) | (block_of(source) == far), factor * drawn, drawn)


def levels(key, shape, cuts, low, high):
    level = 1.0
    for position, parts in cuts:
        steps = jax.random.uniform(jax.random.fold_in(jax.random.fold_in(key, 6), position), (parts,), jnp.float32, low / len(cuts), high / len(cuts))
        level = level * jnp.repeat(jnp.exp(steps), shape[position] // parts).reshape((-1,) + (1,) * (len(shape) - 1 - position))
    return level


def noise(own_key, shape, deviation, reach, cuts=(), held_as=jnp.bfloat16):
    result = deviation * jax.random.normal(own_key, shape, jnp.float32)
    if cuts:
        result = result * levels(own_key, shape, cuts, -0.22, 0.18)
    return jnp.clip(result, -reach, reach).astype(held_as)


def noise_with(stream_key, shape, deviation, most, cuts, heavy, held_as=jnp.bfloat16):
    entries = deviation * jax.random.normal(stream_key, shape, jnp.float32)
    if cuts:
        entries = entries * levels(stream_key, shape, cuts, -0.22, 0.18)
    return jnp.clip(spiked(entries, jax.random.fold_in(stream_key, 3), *heavy), -most, most).astype(held_as)


def setup_inputs(seed: int = 0) -> dict:
    splits = jax.random.split(jax.random.key(seed), 10)
    grad_parts = noise_with(splits[0], (N_SHARD, BLOCKS, LAYERS, BLOCK, D), 0.045, 1.0, ((0, 2), (1, 4), (2, 4)), (0, 3, 2, 2.0), jnp.float32)
    master = noise(splits[1], (BLOCK, MATS, D), BLOCK ** -0.5, 0.1875, ((0, 16), (1, 2)), jnp.float32)
    owner_map = draw_owner_map(jax.random.fold_in(splits[9], 71), 0)
    left_factor = draw_left_factor(jax.random.fold_in(splits[9], 71), 0)
    right_factor = draw_right_factor(jax.random.fold_in(splits[9], 71), 0)
    left_basis = noise(splits[5], (MATS, BLOCK, BLOCK), BLOCK ** -0.5, 0.1875, ((0, 2), (1, 16)), jnp.float32)
    right_basis = noise(splits[6], (MATS, D, D), D ** -0.5, 0.1875, ((0, 2), (2, 16)), jnp.float32)
    moment_one = noise(splits[7], (MATS, BLOCK, D), 0.2, 3.0, ((0, 2), (1, 16)), jnp.float32)
    moment_two = jnp.clip(jnp.exp(math.log(0.5) - 3.912023 * jax.random.uniform(splits[8], (MATS, BLOCK, D), jnp.float32) ** levels(splits[8], (MATS, BLOCK, D), ((0, 2), (1, 16)), -0.2, 0.2)), 0.01, 0.5)
    return {"grad_parts": grad_parts, "master": master, "owner_map": owner_map, "left_factor": left_factor, "right_factor": right_factor, "left_basis": left_basis, "right_basis": right_basis, "moment_one": moment_one, "moment_two": moment_two}


beta_one = 0.95
beta_two = 0.95
epsilon = 1e-08
learn_rate = 0.01
decay_weight = 0.1
step_count = 10

def slot_table(owner_map, shards):
    owners_flat = owner_map.reshape(-1).astype(jnp.int32)
    matrices = owners_flat.shape[0]
    per_owner = matrices // shards
    member = (owners_flat[:, None] == jnp.arange(shards, dtype=jnp.int32)[None, :]).astype(jnp.int32)
    before = jnp.cumsum(member, axis=0) - member
    rank_in = lax.optimization_barrier(jnp.sum(before * member, axis=1)).astype(jnp.int32)
    slot_of = owners_flat * per_owner + rank_in
    places = (slot_of[:, None] == jnp.arange(matrices, dtype=jnp.int32)[None, :]).astype(jnp.int32)
    source = lax.optimization_barrier(jnp.sum(places * jnp.arange(matrices, dtype=jnp.int32)[:, None], axis=0)).astype(jnp.int32)
    return (slot_of, source)

def reference(grad_parts, master, owner_map, left_factor, right_factor, left_basis, right_basis, moment_one, moment_two):
    exact_mode = lax.Precision.HIGHEST
    summed = lax.optimization_barrier(jnp.sum(grad_parts, axis=0))
    matrices = summed.reshape(MATS, BLOCK, D)
    slot_of, source = slot_table(owner_map, N_SHARD)
    slot_grads = jnp.take(matrices, source, axis=0)
    new_left = beta_two * left_factor + (1.0 - beta_two) * jnp.einsum('qfn,qkn->qfk', slot_grads, slot_grads, precision=exact_mode)
    new_right = beta_two * right_factor + (1.0 - beta_two) * jnp.einsum('qfc,qfn->qcn', slot_grads, slot_grads, precision=exact_mode)
    turned = jnp.einsum('qrf,qfn->qrn', left_basis, slot_grads, precision=exact_mode)
    rotated = jnp.einsum('qrn,qnk->qrk', turned, right_basis, precision=exact_mode)
    new_moment_one = beta_one * moment_one + (1.0 - beta_one) * rotated
    new_moment_two = beta_two * moment_two + (1.0 - beta_two) * rotated * rotated
    first_fix = 1.0 - beta_one ** step_count
    second_fix = 1.0 - beta_two ** step_count
    scaled = new_moment_one / first_fix / (jnp.sqrt(new_moment_two / second_fix) + epsilon)
    pulled = jnp.einsum('qrn,qkn->qrk', scaled, right_basis, precision=exact_mode)
    update = jnp.einsum('qrf,qrk->fqk', left_basis, pulled, precision=exact_mode)
    new_master = master - learn_rate * (update + decay_weight * master)
    return (new_master, update, new_left, new_right, new_moment_one, new_moment_two)
```

```python
import jax
import jax.numpy as jnp
from jax import lax
from jax.sharding import PartitionSpec as P

beta_one = 0.95
beta_two = 0.95
epsilon = 1e-08
learn_rate = 0.01
decay_weight = 0.1
step_count = 10


def slot_table(owner_map, shards):
    owners_flat = owner_map.reshape(-1)
    matrices = owners_flat.shape[0]
    per_owner = matrices // shards
    member = (owners_flat[:, None] == jnp.arange(shards, dtype=jnp.int32)[None, :]).astype(
        jnp.int32
    )
    before = jnp.cumsum(member, axis=0) - member
    rank_in = jnp.sum(before * member, axis=1)
    slot_of = owners_flat * per_owner + rank_in
    places = (slot_of[:, None] == jnp.arange(matrices, dtype=jnp.int32)[None, :]).astype(jnp.int32)
    source = jnp.sum(places * jnp.arange(matrices, dtype=jnp.int32)[:, None], axis=0)
    return (slot_of, source)


def local(
    grad_parts,
    master,
    owner_map,
    left_factor,
    right_factor,
    left_basis,
    right_basis,
    moment_one,
    moment_two,
):
    exact_mode = lax.Precision.HIGHEST
    shards = lax.axis_size("shard")
    members = lax.axis_size(("tensor", "section"))
    position = lax.axis_index(("tensor", "section"))
    slot_of, source = slot_table(owner_map, shards)
    height = left_basis.shape[2]
    width = right_basis.shape[1]
    row_block = height // members
    col_block = width // members
    local_part = grad_parts[0, 0, 0]
    row_piece = lax.psum_scatter(local_part, "shard", scatter_dimension=0, tiled=True)
    stacked = lax.all_gather(row_piece[None], ("tensor", "section"), axis=0, tiled=True)
    ordered = jnp.take(stacked, source, axis=0)
    full_grad = lax.all_to_all(ordered, "shard", split_axis=0, concat_axis=1, tiled=True)
    full_right = lax.all_gather(right_basis, ("tensor", "section"), axis=2, tiled=True)
    grad_band = lax.dynamic_slice_in_dim(full_grad, position * row_block, row_block, 1)
    grad_slab = lax.dynamic_slice_in_dim(full_grad, position * col_block, col_block, 2)
    new_left = beta_two * left_factor + (1.0 - beta_two) * jnp.einsum(
        "orn,ofn->orf", grad_band, full_grad, precision=exact_mode
    )
    new_right = beta_two * right_factor + (1.0 - beta_two) * jnp.einsum(
        "ofc,ofn->ocn", grad_slab, full_grad, precision=exact_mode
    )
    turned = jnp.einsum("orf,ofn->orn", left_basis, full_grad, precision=exact_mode)
    rotated = jnp.einsum("orn,onk->ork", turned, full_right, precision=exact_mode)
    new_moment_one = beta_one * moment_one + (1.0 - beta_one) * rotated
    new_moment_two = beta_two * moment_two + (1.0 - beta_two) * rotated * rotated
    first_fix = 1.0 - beta_one**step_count
    second_fix = 1.0 - beta_two**step_count
    scaled = new_moment_one / first_fix / (jnp.sqrt(new_moment_two / second_fix) + epsilon)
    pulled = jnp.einsum("orn,okn->ork", scaled, full_right, precision=exact_mode)
    update_dir = lax.psum_scatter(
        jnp.einsum("orf,ork->fok", left_basis, pulled, precision=exact_mode),
        ("tensor", "section"),
        scatter_dimension=0,
        tiled=True,
    )
    new_master = master - learn_rate * (update_dir + decay_weight * master)
    return (new_master, update_dir, new_left, new_right, new_moment_one, new_moment_two)


def slotwise(
    grad_parts,
    master,
    owner_map,
    left_factor,
    right_factor,
    left_basis,
    right_basis,
    moment_one,
    moment_two,
):
    mode = lax.Precision.HIGH
    group = ("major", "section")
    everyone = ("major", "minor", "section")
    shards = lax.axis_size("shard")
    majors = lax.axis_size("major")
    sections = lax.axis_size("section")
    members = 2 * majors * sections
    slots = members // 2
    side = lax.axis_index("minor")
    _, source = slot_table(owner_map, shards)
    height = left_basis.shape[2]
    width = right_basis.shape[1]
    rows = height // members
    cols = width // members
    part = width // shards

    def swap(bands):
        return lax.all_to_all(bands, group, split_axis=0, concat_axis=0, tiled=True)

    def natural(gathered):
        split = gathered.reshape((2, majors, sections) + gathered.shape[2:])
        return jnp.swapaxes(split, 0, 1)

    summed = lax.psum_scatter(grad_parts[0, 0, 0], "shard", scatter_dimension=1, tiled=True)
    pieces = lax.all_to_all(
        summed.reshape(members, rows, part), everyone, split_axis=0, concat_axis=0, tiled=True
    )
    ordered = jnp.take(pieces, source, axis=0)
    mine = lax.all_to_all(ordered, "shard", split_axis=0, concat_axis=0, tiled=True)
    mine = jnp.swapaxes(mine.reshape(shards, slots, rows, part), 0, 1)
    bands = swap(mine)
    whole = natural(lax.all_gather(bands, "minor", axis=0))
    grad = jnp.swapaxes(whole, 3, 4).reshape(height, width)

    left_half = swap(left_basis).reshape(height // 2, height)
    left_full = lax.all_gather(left_half, "minor", axis=0)
    right_half = swap(jnp.swapaxes(right_basis, 1, 2))
    right_turned = natural(lax.all_gather(right_half, "minor", axis=0)).reshape(width, width)

    turned = jnp.einsum("rf,fn->rn", left_half, grad, precision=mode)
    rotated_half = jnp.einsum("rn,kn->rk", turned, right_turned, precision=mode)
    rotated = swap(rotated_half.reshape(slots, rows, width))
    new_moment_one = beta_one * moment_one + (1.0 - beta_one) * rotated
    new_moment_two = beta_two * moment_two + (1.0 - beta_two) * rotated * rotated
    first_fix = 1.0 - beta_one**step_count
    second_fix = 1.0 - beta_two**step_count
    scaled = new_moment_one / first_fix / (jnp.sqrt(new_moment_two / second_fix) + epsilon)
    scaled_half = swap(scaled).reshape(height // 2, width)

    band_rows = lax.dynamic_index_in_dim(
        grad.reshape(majors, 2, sections * rows, width), side, 1, keepdims=False
    ).reshape(height // 2, width)
    left_product = jnp.einsum("rn,fn->rf", band_rows, grad, precision=mode)
    band_cols = lax.dynamic_index_in_dim(
        grad.reshape(height, majors, 2, sections * cols), side, 2, keepdims=False
    ).reshape(height, width // 2)
    right_product = jnp.einsum("fc,fn->cn", band_cols, grad, precision=mode)
    new_left = beta_two * left_factor + (1.0 - beta_two) * swap(
        left_product.reshape(slots, rows, height)
    )
    new_right = beta_two * right_factor + (1.0 - beta_two) * swap(
        right_product.reshape(slots, cols, width)
    )

    pulled_half = jnp.einsum("rk,kn->rn", scaled_half, right_turned, precision=mode)
    pulled = lax.all_gather(pulled_half, "minor", axis=0)
    left_cols = lax.dynamic_index_in_dim(
        left_full.reshape(height, majors, 2, sections * rows), side, 2, keepdims=False
    ).reshape(height, height // 2)
    update_half = jnp.einsum(
        "rf,rn->fn", left_cols, pulled.reshape(height, width), precision=mode
    )
    update_dir = jnp.swapaxes(swap(update_half.reshape(slots, rows, width)), 0, 1)
    new_master = master - learn_rate * (update_dir + decay_weight * master)
    return (new_master, update_dir, new_left, new_right, new_moment_one, new_moment_two)


def solution(mesh):
    shards, tensors, sections = (mesh.shape[name] for name in ("shard", "tensor", "section"))

    def run(*operands):
        own = operands[3].shape[0] // shards
        paired = tensors % 2 == 0 and 2 * own == tensors * sections
        if paired:
            shape = (shards, tensors // 2, 2, sections)
            grid = jax.sharding.Mesh(
                mesh.devices.reshape(shape), ("shard", "major", "minor", "section")
            )
            body, tensor = slotwise, ("major", "minor")
        else:
            grid, body, tensor = mesh, local, ("tensor",)
        band = tensor + ("section",)
        placed = (
            P("shard", tensor, "section", None, None),
            P(band, "shard", None),
            P(),
            P("shard", band, None),
            P("shard", band, None),
            P("shard", band, None),
            P("shard", None, band),
            P("shard", band, None),
            P("shard", band, None),
        )
        results = (placed[1], placed[1], placed[3], placed[4], placed[7], placed[8])
        return jax.shard_map(
            body, mesh=grid, in_specs=placed, out_specs=results, check_vma=False
        )(*operands)

    return run
```

```python
import jax
import jax.numpy as jnp
from jax import lax
from jax.sharding import PartitionSpec as P

beta_one = 0.95
beta_two = 0.95
epsilon = 1e-08
learn_rate = 0.01
decay_weight = 0.1
step_count = 10


def slot_table(owner_map, shards):
    owners_flat = owner_map.reshape(-1)
    matrices = owners_flat.shape[0]
    per_owner = matrices // shards
    member = (owners_flat[:, None] == jnp.arange(shards, dtype=jnp.int32)[None, :]).astype(
        jnp.int32
    )
    before = jnp.cumsum(member, axis=0) - member
    rank_in = jnp.sum(before * member, axis=1)
    slot_of = owners_flat * per_owner + rank_in
    places = (slot_of[:, None] == jnp.arange(matrices, dtype=jnp.int32)[None, :]).astype(jnp.int32)
    source = jnp.sum(places * jnp.arange(matrices, dtype=jnp.int32)[:, None], axis=0)
    return (slot_of, source)


def local(
    grad_parts,
    master,
    owner_map,
    left_factor,
    right_factor,
    left_basis,
    right_basis,
    moment_one,
    moment_two,
):
    exact_mode = lax.Precision.HIGHEST
    shards = lax.axis_size("shard")
    members = lax.axis_size(("tensor", "section"))
    position = lax.axis_index(("tensor", "section"))
    slot_of, source = slot_table(owner_map, shards)
    height = left_basis.shape[2]
    width = right_basis.shape[1]
    row_block = height // members
    col_block = width // members
    local_part = grad_parts[0, 0, 0]
    row_piece = lax.psum_scatter(local_part, "shard", scatter_dimension=0, tiled=True)
    stacked = lax.all_gather(row_piece[None], ("tensor", "section"), axis=0, tiled=True)
    ordered = jnp.take(stacked, source, axis=0)
    full_grad = lax.all_to_all(ordered, "shard", split_axis=0, concat_axis=1, tiled=True)
    full_right = lax.all_gather(right_basis, ("tensor", "section"), axis=2, tiled=True)
    grad_band = lax.dynamic_slice_in_dim(full_grad, position * row_block, row_block, 1)
    grad_slab = lax.dynamic_slice_in_dim(full_grad, position * col_block, col_block, 2)
    new_left = beta_two * left_factor + (1.0 - beta_two) * jnp.einsum(
        "orn,ofn->orf", grad_band, full_grad, precision=exact_mode
    )
    new_right = beta_two * right_factor + (1.0 - beta_two) * jnp.einsum(
        "ofc,ofn->ocn", grad_slab, full_grad, precision=exact_mode
    )
    turned = jnp.einsum("orf,ofn->orn", left_basis, full_grad, precision=exact_mode)
    rotated = jnp.einsum("orn,onk->ork", turned, full_right, precision=exact_mode)
    new_moment_one = beta_one * moment_one + (1.0 - beta_one) * rotated
    new_moment_two = beta_two * moment_two + (1.0 - beta_two) * rotated * rotated
    first_fix = 1.0 - beta_one**step_count
    second_fix = 1.0 - beta_two**step_count
    scaled = new_moment_one / first_fix / (jnp.sqrt(new_moment_two / second_fix) + epsilon)
    pulled = jnp.einsum("orn,okn->ork", scaled, full_right, precision=exact_mode)
    update_dir = lax.psum_scatter(
        jnp.einsum("orf,ork->fok", left_basis, pulled, precision=exact_mode),
        ("tensor", "section"),
        scatter_dimension=0,
        tiled=True,
    )
    new_master = master - learn_rate * (update_dir + decay_weight * master)
    return (new_master, update_dir, new_left, new_right, new_moment_one, new_moment_two)


def slotwise(
    grad_parts,
    master,
    owner_map,
    left_factor,
    right_factor,
    left_basis,
    right_basis,
    moment_one,
    moment_two,
):
    mode = lax.Precision.HIGH
    group = ("major", "section")
    everyone = ("major", "minor", "section")
    shards = lax.axis_size("shard")
    majors = lax.axis_size("major")
    sections = lax.axis_size("section")
    members = 2 * majors * sections
    slots = members // 2
    side = lax.axis_index("minor")
    _, source = slot_table(owner_map, shards)
    height = left_basis.shape[2]
    width = right_basis.shape[1]
    rows = height // members
    cols = width // members
    part = width // shards

    def swap(bands):
        return lax.all_to_all(bands, group, split_axis=0, concat_axis=0, tiled=True)

    def across(axis, value):
        return lax.ppermute(value, axis, [(0, 1), (1, 0)])

    def in_order(index, own, other, axis):
        lower = jnp.where(index == 0, own, other)
        upper = jnp.where(index == 0, other, own)
        return jnp.stack((lower, upper), axis=axis)

    def natural(own, other):
        shape = (majors, sections) + own.shape[1:]
        return in_order(side, own.reshape(shape), other.reshape(shape), 1)

    me = lax.axis_index("shard")
    partial = grad_parts[0, 0, 0]
    kept = lax.dynamic_slice_in_dim(partial, me * part, part, 1)
    crossing = across("shard", lax.dynamic_slice_in_dim(partial, (1 - me) * part, part, 1))
    left_half = swap(left_basis)
    crossing, left_half = lax.optimization_barrier((crossing, left_half))
    summed = kept + crossing
    pieces = lax.all_to_all(
        summed.reshape(members, rows, part), everyone, split_axis=0, concat_axis=0, tiled=True
    )
    right_bands = jnp.swapaxes(right_basis, 1, 2)
    pieces, right_bands = lax.optimization_barrier((pieces, right_bands))
    theirs = jnp.take(pieces, lax.dynamic_slice_in_dim(source, (1 - me) * slots, slots), axis=0)
    ours = jnp.take(pieces, lax.dynamic_slice_in_dim(source, me * slots, slots), axis=0)
    arrived = across("shard", theirs)
    right_half = swap(right_bands)
    arrived, right_half = lax.optimization_barrier((arrived, right_half))
    bands = swap(in_order(me, ours, arrived, 1))
    whole = natural(bands, across("minor", bands))
    grad = jnp.swapaxes(whole, 3, 4).reshape(height, width)
    right_turned = natural(right_half, across("minor", right_half)).reshape(width, width)
    left_other = across("minor", left_half).reshape(height // 2, height)
    left_half = left_half.reshape(height // 2, height)

    turned = jnp.einsum("rf,fn->rn", left_half, grad, precision=mode)
    rotated_half = jnp.einsum("rn,kn->rk", turned, right_turned, precision=mode)
    band_rows = lax.dynamic_index_in_dim(
        grad.reshape(majors, 2, sections * rows, width), side, 1, keepdims=False
    ).reshape(height // 2, width)
    left_product = jnp.einsum("rn,fn->rf", band_rows, grad, precision=mode)
    band_cols = lax.dynamic_index_in_dim(
        grad.reshape(height, majors, 2, sections * cols), side, 2, keepdims=False
    ).reshape(height, width // 2)
    right_product = jnp.einsum("fc,fn->cn", band_cols, grad, precision=mode)
    rotated = swap(rotated_half.reshape(slots, rows, width))
    rotated, left_product, right_product = lax.optimization_barrier(
        (rotated, left_product, right_product)
    )
    new_moment_one = beta_one * moment_one + (1.0 - beta_one) * rotated
    new_moment_two = beta_two * moment_two + (1.0 - beta_two) * rotated * rotated
    first_fix = 1.0 - beta_one**step_count
    second_fix = 1.0 - beta_two**step_count
    scaled = new_moment_one / first_fix / (jnp.sqrt(new_moment_two / second_fix) + epsilon)
    scaled_half = swap(scaled).reshape(height // 2, width)

    new_left = beta_two * left_factor + (1.0 - beta_two) * swap(
        left_product.reshape(slots, rows, height)
    )
    new_right = beta_two * right_factor + (1.0 - beta_two) * swap(
        right_product.reshape(slots, cols, width)
    )

    pulled_half = jnp.einsum("rk,kn->rn", scaled_half, right_turned, precision=mode)
    pulled_other = across("minor", pulled_half)

    def my_columns(half):
        split = half.reshape(height // 2, majors, 2, sections * rows)
        return lax.dynamic_index_in_dim(split, side, 2, keepdims=False).reshape(
            height // 2, height // 2
        )

    update_half = jnp.einsum(
        "rf,rn->fn", my_columns(left_half), pulled_half, precision=mode
    ) + jnp.einsum("rf,rn->fn", my_columns(left_other), pulled_other, precision=mode)
    update_dir = jnp.swapaxes(swap(update_half.reshape(slots, rows, width)), 0, 1)
    new_master = master - learn_rate * (update_dir + decay_weight * master)
    return (new_master, update_dir, new_left, new_right, new_moment_one, new_moment_two)


def solution(mesh):
    shards, tensors, sections = (mesh.shape[name] for name in ("shard", "tensor", "section"))

    def run(*operands):
        own = operands[3].shape[0] // shards
        paired = shards == 2 and tensors % 2 == 0 and 2 * own == tensors * sections
        if paired:
            shape = (shards, tensors // 2, 2, sections)
            grid = jax.sharding.Mesh(
                mesh.devices.reshape(shape), ("shard", "major", "minor", "section")
            )
            body, tensor = slotwise, ("major", "minor")
        else:
            grid, body, tensor = mesh, local, ("tensor",)
        band = tensor + ("section",)
        placed = (
            P("shard", tensor, "section", None, None),
            P(band, "shard", None),
            P(),
            P("shard", band, None),
            P("shard", band, None),
            P("shard", band, None),
            P("shard", None, band),
            P("shard", band, None),
            P("shard", band, None),
        )
        results = (placed[1], placed[1], placed[3], placed[4], placed[7], placed[8])
        return jax.shard_map(
            body, mesh=grid, in_specs=placed, out_specs=results, check_vma=False
        )(*operands)

    return run
```
